32 devices in a mesh: groups: 2 (over y), seq: 16 (over z, x, core).
Axes of the slice: x: 2, y: 2, z: 4, core: 2. Of those that a mesh axis runs over, the one named last changes fastest.
Arguments:
- features: bfloat16 [2, 16384, 1408], P('groups', 'seq'), parts along dimension 0, may hold values from -600 to 600
- norm_gain: float32 [1408], replicated, may hold values from 0.1 to 1.9
- conv_weight: bfloat16 [5, 1408, 1536], P(None, None, 'seq'), may hold values from -0.0625 to 0.0625
- pair_projection: bfloat16 [1536, 512], replicated, may hold values from -0.15625 to 0.15625
- outer_weight: bfloat16 [128, 128], replicated, may hold values from -0.5 to 0.5
- row_gate: bfloat16 [128, 128], replicated, may hold values from -0.5 to 0.5
- row_output: bfloat16 [128, 128], replicated, may hold values from -0.5 to 0.5
- column_gate: bfloat16 [128, 128], replicated, may hold values from -0.5 to 0.5
- column_output: bfloat16 [128, 128], replicated, may hold values from -0.5 to 0.5
Outputs:
- trunk: bfloat16 [2, 8192, 1536], P('groups', 'seq'), parts along dimension 0
- pair: bfloat16 [2, 512, 512, 128], P('groups', 'seq'), parts along dimension 0
The draws below stay inside these ranges and needn't reach their ends.
There are 2 independent parts, one for each index of `groups`. The reference program is written for one: setup_inputs(seed, part) draws one part's arguments, and reference() takes and returns one part's arrays. A program takes and returns all parts, laid end to end along the dimension named above; an argument that names none is the same for every part. Nothing has to cross between parts.
All inputs are finite; a program needn't handle non-finite values.
Results may differ from the reference program's by a relative error of at most 0.0095.
Values may be sent and summed in bfloat16 or wider, within the bound.
No kernel may reach another device: no remote copies, remote signals or barrier semaphores. Data moves between devices by JAX's collectives and lax.ppermute only.
A program may use at most 192 MiB of HBM per device.

```python
import math
import jax
import jax.numpy as jnp
from jax import lax

CIN = 1408
COUT = 1536
CP = 128
KW = 5
TOK = 512
W = 1
LEN = 16384
HALF = 8192
SPAN = 256


def draw_features(key, part):
    first, second, third = jax.random.split(key, 3)
    base = jnp.clip(jax.random.normal(first, (W, LEN, CIN), jnp.float32), -6.0, 6.0)
    row_scale = jnp.exp(jax.random.uniform(second, (W, LEN, 1), jnp.float32, 0.0, math.log(10.0)))
    channel_scale = jnp.exp(jax.random.uniform(third, (1, 1, CIN), jnp.float32, 0.0, math.log(10.0)))
    return (base * row_scale * channel_scale).astype(jnp.bfloat16)


def levels(stream_key, shape, shards, smallest, largest):
    def one(dim, blocks):
        heights = jax.random.uniform(jax.random.fold_in(jax.random.fold_in(stream_key, 6), dim), (blocks,), jnp.float32, smallest / len(shards), largest / len(shards))
        return jnp.repeat(jnp.exp(heights), shape[dim] // blocks).reshape((-1,) + (1,) * (len(shape) - dim - 1))

    gain = one(*shards[0])
    for cut in shards[1:]:
        gain = gain * one(*cut)
    return gain


def centred(key, shape, deviation, most, pieces=(), kind=jnp.bfloat16):
    loudness = levels(key, shape, pieces, -0.22, 0.18) if pieces else 1.0
    drawn = jax.random.normal(key, shape, jnp.float32) * deviation * loudness
    return jnp.minimum(jnp.maximum(drawn, -most), most).astype(kind)


def setup_inputs(seed: int = 0, part: int = 0) -> dict:
    keys = jax.random.split(jax.random.key(seed), 10)
    part_keys = jax.random.split(jax.random.fold_in(keys[9], part), 10)
    return {
        "features": draw_features(jax.random.fold_in(jax.random.fold_in(keys[9], part), 71), part),
        "norm_gain": jnp.clip(1.0 + 0.18 * jax.random.normal(keys[1], (CIN,), jnp.float32), 0.1, 1.9),
        "conv_weight": centred(keys[2], (KW, CIN, COUT), (KW * CIN) ** -0.5, 0.0625, ((2, 16),)),
        "pair_projection": centred(keys[3], (COUT, 4 * CP), COUT ** -0.5, 0.15625),
        "outer_weight": centred(keys[4], (CP, CP), CP ** -0.5, 0.5),
        "row_gate": centred(keys[5], (CP, CP), CP ** -0.5, 0.5),
        "row_output": centred(keys[6], (CP, CP), CP ** -0.5, 0.5),
        "column_gate": centred(keys[7], (CP, CP), CP ** -0.5, 0.5),
        "column_output": centred(keys[8], (CP, CP), CP ** -0.5, 0.5),
    }


def layer_norm(values):
    center = values - lax.optimization_barrier(jnp.mean(values, axis=-1, keepdims=True))
    return center * lax.rsqrt(lax.optimization_barrier(jnp.mean(center * center, axis=-1, keepdims=True)) + 1e-05)

def distance_kernel(row_index, column_index, reach):
    return jnp.exp(-jnp.abs(row_index[:, None] - column_index[None, :]) / reach).astype(jnp.bfloat16)

def reference(features, norm_gain, conv_weight, pair_projection, outer_weight, row_gate, row_output, column_gate, column_output):
    positions = jnp.arange(TOK, dtype=jnp.float32)
    kernel = distance_kernel(positions, positions, jnp.float32(SPAN)).astype(jnp.float32)
    row_total = lax.optimization_barrier(jnp.sum(kernel, axis=1))
    column_total = lax.optimization_barrier(jnp.sum(kernel, axis=0))
    filters = conv_weight.astype(jnp.float32)
    gains = norm_gain.astype(jnp.float32)
    highest = lax.Precision.HIGHEST

    def window(sample):
        values = sample.astype(jnp.float32)
        scaled = values * lax.rsqrt(lax.optimization_barrier(jnp.mean(values * values, axis=-1, keepdims=True)) + 1e-06) * gains
        activated = jax.nn.gelu(scaled).astype(jnp.bfloat16)
        padded = jnp.pad(activated.astype(jnp.float32), ((KW // 2, KW // 2), (0, 0)))
        convolved = jnp.zeros((LEN, COUT), jnp.float32)
        for offset in range(KW):
            convolved = convolved + jnp.dot(padded[offset:offset + LEN], filters[offset], precision=highest)
        trunk = lax.optimization_barrier(jnp.max(convolved.reshape(HALF, 2, COUT), axis=1)).astype(jnp.bfloat16)
        tokens = lax.optimization_barrier(jnp.mean(trunk.astype(jnp.float32).reshape(TOK, HALF // TOK, COUT), axis=1)).astype(jnp.bfloat16)
        projected = jnp.dot(tokens, pair_projection, preferred_element_type=jnp.float32)
        left = projected[:, :CP]
        right = projected[:, CP:2 * CP].astype(jnp.bfloat16)
        start_term = projected[:, 2 * CP:3 * CP]
        end_term = projected[:, 3 * CP:].astype(jnp.bfloat16)
        outer = (left[:, None, :] * right.astype(jnp.float32)[None, :, :]).astype(jnp.bfloat16)
        initial = jnp.einsum('ijc,cd->ijd', outer.astype(jnp.float32), outer_weight.astype(jnp.float32), precision=highest)
        initial = initial + start_term[:, None, :] + end_term.astype(jnp.float32)[None, :, :]
        normed = layer_norm(initial).astype(jnp.bfloat16).astype(jnp.float32)
        row_mean = (jnp.einsum('ij,ijc->ic', kernel, normed, precision=highest) / row_total[:, None]).astype(jnp.bfloat16)
        row_term = jnp.dot(row_mean, row_output, preferred_element_type=jnp.float32)
        row_weight = jax.nn.sigmoid(jnp.einsum('ijc,cd->ijd', normed, row_gate.astype(jnp.float32), precision=highest))
        after_rows = (initial + row_weight * row_term[:, None, :]).astype(jnp.bfloat16)
        column_normed = layer_norm(after_rows.astype(jnp.float32)).astype(jnp.bfloat16).astype(jnp.float32)
        column_mean = (jnp.einsum('ij,ijc->jc', kernel, column_normed, precision=highest) / column_total[:, None]).astype(jnp.bfloat16)
        column_term = jnp.dot(column_mean, column_output, preferred_element_type=jnp.float32)
        column_weight = jax.nn.sigmoid(jnp.einsum('ijc,cd->ijd', column_normed, column_gate.astype(jnp.float32), precision=highest))
        pair = (after_rows.astype(jnp.float32) + column_weight * column_term[None, :, :]).astype(jnp.bfloat16)
        return (trunk, pair)
    trunk, pair = lax.map(window, features)
    return (trunk, pair)
```

```python
import jax
import jax.numpy as jnp
from jax import lax
from jax.experimental import pallas as pl
from jax.experimental.pallas import tpu as pltpu
from jax.sharding import PartitionSpec as P

KW = 5
F32 = jnp.float32
BF16 = jnp.bfloat16


def layer_norm(values):
    center = values - jnp.mean(values, axis=-1, keepdims=True)
    return center * lax.rsqrt(jnp.mean(center * center, axis=-1, keepdims=True) + 1e-05)


def distance_kernel(row_index, column_index, reach):
    return jnp.exp(-jnp.abs(row_index[:, None] - column_index[None, :]) / reach).astype(BF16)


NT = (((1,), (1,)), ((), ()))


def tap_kernel(first, tap_ref, even_ref, odd_ref, weight_ref, *refs):
    out_ref = refs[-1]
    weight = weight_ref[...]
    for parity, rows in enumerate((even_ref, odd_ref)):
        part = lax.dot_general(rows[0], weight, NT, preferred_element_type=F32)
        if first:
            out_ref[parity] = part
        else:
            out_ref[parity] = refs[0][parity] + part


def conv_tap(stack, tap, column, weight, total, width, block):
    _, rows, depth = stack.shape
    count = weight.shape[0] // block
    scalars = jnp.stack([tap, column]).astype(jnp.int32)
    total_spec = pl.BlockSpec((2, rows, block), lambda j, s: (0, 0, s[1] * count + j))
    in_specs = [
        pl.BlockSpec((1, rows, depth), lambda j, s: (s[0], 0, 0)),
        pl.BlockSpec((1, rows, depth), lambda j, s: (s[0] + 1, 0, 0)),
        pl.BlockSpec((block, depth), lambda j, s: (j, 0)),
    ]
    args = [scalars, stack, stack, weight]
    aliases = {}
    if total is not None:
        in_specs.append(total_spec)
        args.append(total)
        aliases = {4: 0}
    return pl.pallas_call(
        lambda *refs: tap_kernel(total is None, *refs),
        out_shape=jax.ShapeDtypeStruct((2, rows, width), F32),
        grid_spec=pltpu.PrefetchScalarGridSpec(
            num_scalar_prefetch=1, grid=(count,), in_specs=in_specs, out_specs=total_spec
        ),
        input_output_aliases=aliases,
        compiler_params=pltpu.CompilerParams(dimension_semantics=("arbitrary",)),
        cost_estimate=pl.CostEstimate(
            flops=4 * rows * depth * weight.shape[0],
            bytes_accessed=2 * weight.size + 16 * rows * weight.shape[0],
            transcendentals=0,
        ),
        name="conv_tap",
    )(*args)


def last_kernel(even_ref, odd_ref, weight_ref, total_ref, proj_ref, trunk_ref, out_ref):
    weight = weight_ref[...]
    even = total_ref[0] + lax.dot_general(even_ref[...], weight, NT, preferred_element_type=F32)
    odd = total_ref[1] + lax.dot_general(odd_ref[...], weight, NT, preferred_element_type=F32)
    trunk = jnp.maximum(even, odd).astype(BF16)
    trunk_ref[...] = trunk
    rows, block = trunk.shape
    tokens = jnp.mean(trunk.astype(F32).reshape(rows // 16, 16, block), axis=1).astype(BF16)
    part = jnp.dot(tokens, proj_ref[...], preferred_element_type=F32)

    @pl.when(pl.program_id(0) == 0)
    def _():
        out_ref[...] = part

    @pl.when(pl.program_id(0) != 0)
    def _():
        out_ref[...] += part


def conv_last(even, odd, weight, total, projection, block):
    rows, depth = even.shape
    width = weight.shape[0]
    terms = projection.shape[1]
    return pl.pallas_call(
        last_kernel,
        grid=(width // block,),
        in_specs=[
            pl.BlockSpec((rows, depth), lambda j: (0, 0)),
            pl.BlockSpec((rows, depth), lambda j: (0, 0)),
            pl.BlockSpec((block, depth), lambda j: (j, 0)),
            pl.BlockSpec((2, rows, block), lambda j: (0, 0, j)),
            pl.BlockSpec((block, terms), lambda j: (j, 0)),
        ],
        out_specs=[
            pl.BlockSpec((rows, block), lambda j: (0, j)),
            pl.BlockSpec((rows // 16, terms), lambda j: (0, 0)),
        ],
        out_shape=[
            jax.ShapeDtypeStruct((rows, width), BF16),
            jax.ShapeDtypeStruct((rows // 16, terms), F32),
        ],
        compiler_params=pltpu.CompilerParams(dimension_semantics=("arbitrary",)),
        cost_estimate=pl.CostEstimate(
            flops=4 * rows * depth * width,
            bytes_accessed=2 * weight.size + 10 * rows * width,
            transcendentals=0,
        ),
        name="conv_last",
    )(even, odd, weight, total, projection)


class Ring:
    def __init__(self, peers, stride, size):
        self.peers, self.stride, self.size = peers, stride, size

    def place(self):
        return (lax.axis_index("seq") // self.stride) % self.size

    def shift(self, values, step):
        pairs = []
        for i in range(self.peers):
            place = (i // self.stride) % self.size
            other = (place + step) % self.size
            pairs.append((i, i + (other - place) * self.stride))
        return lax.ppermute(values, "seq", pairs)

    def gather(self, values):
        size = self.size
        if size == 2:
            other = self.shift(values, 1)
            mine_first = self.place() == 0
            return jnp.where(
                mine_first,
                jnp.concatenate([values, other], 0),
                jnp.concatenate([other, values], 0),
            )
        length = values.shape[0]
        received = [values] + [self.shift(values, step) for step in range(1, size)]
        ordered = [received[0]] + received[:0:-1]
        twice = jnp.concatenate(ordered + ordered, 0)
        start = (size - self.place()) % size * length
        return lax.dynamic_slice_in_dim(twice, start, size * length, 0)

    def total(self, values):
        narrow = values.astype(BF16)
        for step in range(1, self.size):
            values = values + self.shift(narrow, step).astype(F32)
        return values


def body(
    features,
    norm_gain,
    conv_weight,
    pair_projection,
    outer_weight,
    row_gate,
    row_output,
    column_gate,
    column_output,
    x_size,
):
    peers = lax.axis_size("seq")
    groups = lax.axis_size("groups")
    core_ring = Ring(peers, 1, 2)
    x_ring = Ring(peers, 2, x_size)
    z_ring = Ring(peers, 2 * x_size, peers // (2 * x_size))
    group = lax.axis_index("groups")
    core = core_ring.place()

    filters = jnp.transpose(conv_weight, (0, 2, 1))

    def gathered(part):
        return lax.all_gather(part, "seq", axis=0, tiled=True)

    own_tap = gathered(lax.dynamic_index_in_dim(filters, group, 0, keepdims=False))
    rest = [gathered(filters[tap]) for tap in range(2, KW)]
    width = own_tap.shape[0]
    half = width // 2
    mine = lax.dynamic_slice_in_dim(own_tap, core * half, half, 0)
    swap = [(i, (i + peers) % (2 * peers)) for i in range(2 * peers)]
    near = lax.ppermute(mine, ("groups", "seq"), swap)
    far = core_ring.shift(near, 1)

    local_bins, channels = features.shape[1:]
    bins = features[0]
    up = [(i, i + 1) for i in range(peers - 1)]
    down = [(i + 1, i) for i in range(peers - 1)]
    before = lax.ppermute(bins[local_bins - 2 :], "seq", up)
    after = lax.ppermute(bins[:2], "seq", down)
    values = jnp.concatenate([before, bins, after], axis=0).astype(F32)
    scaled = (
        values * lax.rsqrt(jnp.mean(values * values, axis=-1, keepdims=True) + 1e-06) * norm_gain
    )
    activated = jax.nn.gelu(scaled).astype(BF16)
    pooled = local_bins // 2
    pairs = activated.reshape(pooled + 2, 2, channels)
    stack = jnp.stack([pairs[k // 2 : k // 2 + pooled, k % 2] for k in range(6)])

    block = 256
    total = conv_tap(stack, group, jnp.int32(0), own_tap, None, width, block)
    for tap in range(2, KW - 1):
        total = conv_tap(stack, jnp.int32(tap), jnp.int32(0), rest[tap - 2], total, width, block)
    total = conv_tap(stack, 1 - group, core, near, total, width, block)
    total = conv_tap(stack, 1 - group, 1 - core, far, total, width, block)
    trunk, projected = conv_last(
        stack[KW - 1], stack[KW], rest[-1], total, pair_projection, block
    )
    trunk = trunk[None]

    pair_width = outer_weight.shape[0]
    local_rows = local_bins // 32
    left = projected[:, :pair_width][None]
    start_term = projected[:, 2 * pair_width : 3 * pair_width][None]
    sent = jnp.concatenate(
        [projected[:, pair_width : 2 * pair_width], projected[:, 3 * pair_width :]], axis=1
    ).astype(BF16)
    for ring in (core_ring, x_ring, z_ring):
        sent = ring.gather(sent)
    right = sent[None, :, :pair_width]
    end_term = sent[None, :, pair_width:]
    all_count = right.shape[1]

    outer = (left[:, :, None, :] * right.astype(F32)[:, None, :, :]).astype(BF16)
    initial = jnp.einsum("wijc,cd->wijd", outer, outer_weight, preferred_element_type=F32)
    initial = initial + start_term[:, :, None, :] + end_term.astype(F32)[:, None, :, :]
    reach = jnp.float32(8 * local_rows * peers // 16)
    first_row = lax.axis_index("seq") * local_rows
    own_index = (first_row + jnp.arange(local_rows, dtype=jnp.int32)).astype(F32)
    all_index = jnp.arange(all_count, dtype=F32)
    row_kernel = distance_kernel(own_index, all_index, reach)
    row_total = jnp.sum(row_kernel.astype(F32), axis=1)
    normed = layer_norm(initial).astype(BF16)
    row_mean = (
        jnp.einsum("ij,wijc->wic", row_kernel, normed, preferred_element_type=F32)
        / row_total[None, :, None]
    ).astype(BF16)
    row_term = jnp.einsum("wic,cd->wid", row_mean, row_output, preferred_element_type=F32)
    row_weight = jax.nn.sigmoid(
        jnp.einsum("wijc,cd->wijd", normed, row_gate, preferred_element_type=F32)
    )
    after_rows = (initial + row_weight * row_term[:, :, None, :]).astype(BF16)
    full_kernel = distance_kernel(all_index, all_index, reach)
    column_total = jnp.sum(full_kernel.astype(F32), axis=0)
    column_normed = layer_norm(after_rows.astype(F32)).astype(BF16)
    partial_sums = jnp.einsum(
        "ij,wijc->jc", row_kernel, column_normed, preferred_element_type=F32
    )
    half_count = all_count // 2
    kept = lax.dynamic_slice_in_dim(partial_sums, core * half_count, half_count, 0)
    given = lax.dynamic_slice_in_dim(partial_sums, (1 - core) * half_count, half_count, 0)
    kept = kept + core_ring.shift(given, 1)
    kept = z_ring.total(x_ring.total(kept))
    half_total = lax.dynamic_slice_in_dim(column_total, core * half_count, half_count, 0)
    column_mean = core_ring.gather((kept / half_total[:, None]).astype(BF16))
    column_term = jnp.dot(column_mean, column_output, preferred_element_type=F32)
    column_weight = jax.nn.sigmoid(
        jnp.einsum("wijc,cd->wijd", column_normed, column_gate, preferred_element_type=F32)
    )
    pair = (after_rows.astype(F32) + column_weight * column_term[None, None]).astype(BF16)
    return (trunk, pair)


def solution(mesh):
    places = {getattr(device, "coords", (0,))[0] for device in mesh.devices.flat}
    peers = mesh.shape["seq"]
    x_size = len(places) if len(places) > 1 and peers % (2 * len(places)) == 0 else 2
    in_specs = (P("groups", "seq", None), P(), P(None, None, "seq"), P(), P(), P(), P(), P(), P())
    out_specs = (P("groups", "seq", None), P("groups", "seq", None, None))

    def program(*args):
        return body(*args, x_size)

    return jax.shard_map(
        program, mesh=mesh, in_specs=in_specs, out_specs=out_specs, check_vma=False
    )
```
